32 devices in a mesh: seq: 4 (over z), row: 2 (over x), col: 4 (over y, core).
Axes of the slice: x: 2, y: 2, z: 4, core: 2. Of those that a mesh axis runs over, the one named last changes fastest.
Arguments:
- grads: bfloat16 [1024, 28672], P('row', ('seq', 'col')), may hold values from -6 to 6
- acts: bfloat16 [1024, 8192], P(('seq', 'col'), 'row'), may hold values from -6 to 6
- out_basis: bfloat16 [28672, 28672], P(('seq', 'col'), 'row'), may hold values from -0.03125 to 0.03125
- in_basis: bfloat16 [8192, 8192], P('row', ('seq', 'col')), may hold values from -0.0625 to 0.0625
- lengths: int32 [4], replicated, may hold values from 1 to 256, 768 in all
Outputs:
- eigenvalues: float32 [28672, 8192], P('row', ('seq', 'col'))
The draws below stay inside these ranges and needn't reach their ends.
Inputs may be any that keep to these rules, and one draw needn't show every extreme that they name: lengths sum to 768; some sequence is full.
All inputs are finite; a program needn't handle non-finite values.
Results may differ from the reference program's by a relative error of at most 0.0036.
Values may be sent and summed in bfloat16 or wider, within the bound.
No kernel may reach another device: no remote copies, remote signals or barrier semaphores. Data moves between devices by JAX's collectives and lax.ppermute only.
A program may use at most 192 MiB of HBM per device.

```python
import math
import jax
import jax.numpy as jnp
import numpy as np
from jax import lax

DIN = 8192
DOUT = 28672
SEQ_LEN = 256
SEQS = 4
TOKENS = 1024


def level_of(stream_key, shape, split, least, high):
    factor_of, own = 1.0, jax.random.fold_in(stream_key, 6)
    for dim, shards_of in split:
        steps = jnp.exp(jax.random.uniform(jax.random.fold_in(own, dim), (shards_of,), jnp.float32, least / len(split), high / len(split)))
        factor_of = factor_of * jnp.repeat(steps, shape[dim] // shards_of).reshape([-1 if axis == dim else 1 for axis in range(len(shape))])
    return factor_of


def profile(count, total, reach, slope):
    portions = [(1 << 20) // math.isqrt(standing ** slope) + 1 for standing in range(2, count + 1)]
    surplus, counts = total - reach - (count - 1), [1] * (count - 1)
    while surplus > 0:
        free = [i for i in range(count - 1) if counts[i] < reach]
        pool, budget = sum([portions[i] for i in free]), surplus
        for i in free:
            addition = min(reach - counts[i], max(1, budget * portions[i] // pool), surplus)
            counts[i] = counts[i] + addition
            surplus = surplus - addition
    return np.array([reach] + counts)


def ragged(key, count, total, reach, skew):
    if count == 2:
        one = jax.random.randint(key, (), max(1, total - reach), min(reach, total - 1) + 1)
        return jnp.stack([one, total - one])
    tallies = jnp.asarray(profile(count, total, reach, skew), jnp.int32)
    couples = (count - 1) // 2
    donor, receiver = tallies[1:1 + 2 * couples:2], tallies[2:2 + 2 * couples:2]
    room = jnp.minimum(donor - 1, reach - receiver)
    shifted = jax.random.randint(jax.random.fold_in(key, 1), (couples,), 0, 1 << 20) % (room + 1)
    tallies = tallies.at[1:1 + 2 * couples:2].set(donor - shifted).at[2:2 + 2 * couples:2].set(receiver + shifted)
    return tallies[jax.random.permutation(jax.random.fold_in(key, 2), count)]


def centred(stream_key, dims, scale, most, cuts=(), held_as=jnp.bfloat16):
    result = jax.random.normal(stream_key, dims, jnp.float32) * scale
    if len(cuts) > 0:
        result = level_of(stream_key, dims, cuts, -0.22, 0.18) * result
    return jnp.clip(result, min=-most, max=most).astype(held_as)


def setup_inputs(seed: int = 0) -> dict:
    key_list = jax.random.split(jax.random.key(seed), 6)
    grads = centred(key_list[0], (TOKENS, DOUT), 1.0, 6.0, ((0, 2), (1, 16)))
    acts = centred(key_list[1], (TOKENS, DIN), 1.0, 6.0, ((0, 16), (1, 2)))
    out_basis = centred(key_list[2], (DOUT, DOUT), DOUT ** -0.5, 0.03125, ((0, 16), (1, 2)))
    in_basis = centred(key_list[3], (DIN, DIN), DIN ** -0.5, 0.0625, ((0, 2), (1, 16)))
    lengths = ragged(key_list[4], SEQS, 3 * SEQ_LEN, SEQ_LEN, 2).astype(jnp.int32)
    return dict(grads=grads, acts=acts, out_basis=out_basis, in_basis=in_basis, lengths=lengths)


def reference(grads, acts, out_basis, in_basis, lengths):
    grad_proj = jnp.dot(grads, out_basis, preferred_element_type=jnp.float32).astype(jnp.bfloat16)
    act_full = jnp.dot(acts, in_basis, preferred_element_type=jnp.float32)
    token_index = jnp.arange(TOKENS, dtype=jnp.int32)
    seq_owner = token_index // SEQ_LEN
    position = token_index % SEQ_LEN
    is_live = (position < lengths[seq_owner]).astype(jnp.float32)
    act_proj = (act_full * is_live[:, None]).astype(jnp.bfloat16)
    grad_three = grad_proj.reshape(SEQS, SEQ_LEN, DOUT)
    act_three = act_proj.reshape(SEQS, SEQ_LEN, DIN)

    def accumulate(total, pair):
        grad_seq = lax.dot_general(pair[0], pair[1], (((0,), (0,)), ((), ())), preferred_element_type=jnp.float32)
        return total + grad_seq * grad_seq, None

    total, unused = lax.scan(accumulate, jnp.zeros((DOUT, DIN), jnp.float32), (grad_three, act_three))
    return total / (SEQS * SEQ_LEN)
```

```python
import jax
import jax.numpy as jnp
from jax import lax
from jax.experimental import pallas as pl
from jax.experimental.pallas import tpu as pltpu
from jax.sharding import PartitionSpec as P


SEQ_LEN = 256
WINDOWS = 3
F32 = jnp.float32
BF16 = jnp.bfloat16
PLAN = (1, 2, 2, 2, 2, 2, 2, 1)
PARTS = 14
ORDER = (
    (0, 0), (1, 0), (0, 1), (2, 0), (1, 1), (0, 2), (3, 0), (0, 3), (2, 1), (3, 1),
    (1, 2), (4, 0), (0, 4), (1, 3), (2, 2), (4, 1), (0, 5), (5, 0), (3, 2), (1, 4),
    (2, 3), (5, 1), (6, 0), (4, 2), (1, 5), (0, 6), (3, 3), (6, 1), (0, 7), (2, 4),
    (4, 3), (7, 0), (3, 4), (7, 1), (5, 2), (2, 5), (1, 6), (1, 7), (4, 4), (3, 5),
    (6, 2), (5, 3), (7, 2), (4, 5), (6, 3), (2, 6), (2, 7), (5, 4), (7, 3), (3, 6),
    (6, 4), (3, 7), (5, 5), (7, 4), (4, 6), (4, 7), (6, 5), (7, 5), (5, 6), (5, 7),
    (6, 6), (6, 7), (7, 6), (7, 7),
)


def block_of(width, offset):
    for size in (512, 256, 128):
        if width % size == 0 and offset % size == 0:
            return size
    return width


def dot(lhs, rhs):
    return jnp.dot(lhs, rhs, preferred_element_type=F32)


def cost(flops, moved):
    return pl.CostEstimate(flops=flops, transcendentals=0, bytes_accessed=moved)


def project(where, lhs, basis, offset, width):
    rows = lhs.shape[0] // 4
    depth = lhs.shape[1]
    size = block_of(width, offset)
    start = offset // size

    def kernel(where_ref, lhs_ref, rhs_ref, send_ref, away_ref, own_ref, acc_ref):
        core, side = where_ref[0], where_ref[1]
        acc_ref[...] = dot(lhs_ref[...], rhs_ref[...])

        def quarter(c, s):
            at = pl.multiple_of((2 * c + s) * rows, rows)
            return acc_ref[pl.ds(at, rows), :]

        send_ref[:rows, :] = quarter(1 - core, 1 - side).astype(BF16)
        send_ref[rows:, :] = quarter(1 - core, side).astype(BF16)
        away_ref[...] = quarter(core, 1 - side).astype(BF16)
        own_ref[...] = quarter(core, side).astype(BF16)

    return pl.pallas_call(
        kernel,
        grid_spec=pltpu.PrefetchScalarGridSpec(
            num_scalar_prefetch=1,
            grid=(width // size,),
            in_specs=[
                pl.BlockSpec((4 * rows, depth), lambda i, w: (0, 0)),
                pl.BlockSpec((depth, size), lambda i, w: (0, start + i)),
            ],
            out_specs=[
                pl.BlockSpec((2 * rows, size), lambda i, w: (0, i)),
                pl.BlockSpec((rows, size), lambda i, w: (0, i)),
                pl.BlockSpec((rows, size), lambda i, w: (0, i)),
            ],
            scratch_shapes=[pltpu.VMEM((4 * rows, size), F32)],
        ),
        out_shape=[
            jax.ShapeDtypeStruct((2 * rows, width), BF16),
            jax.ShapeDtypeStruct((rows, width), BF16),
            jax.ShapeDtypeStruct((rows, width), BF16),
        ],
        cost_estimate=cost(8 * rows * depth * width, 2 * depth * width + 8 * rows * width),
    )(where, lhs, basis)


def finish(where, pieces, acts, out, shape, offset, width, scale):
    size = block_of(width, offset)
    start = offset // size
    window = acts[0].shape[0]
    part = window // 8
    columns = shape[1]
    in_specs = [pl.BlockSpec((p.shape[0], size), lambda i, w: (0, i)) for p in pieces]
    in_specs += [pl.BlockSpec(a.shape, lambda i, w: (0, 0)) for a in acts]
    args = [where, *pieces, *acts]
    alias = {}
    if out is not None:
        in_specs.append(pl.BlockSpec(memory_space=pl.ANY))
        alias = {len(args): 0}
        args.append(out)

    def kernel(where_ref, *refs):
        out_ref, proj_ref = refs[-2:]
        core, side, spot = where_ref[0], where_ref[1], where_ref[2]
        for number, piece in enumerate(refs[:4]):
            place = 2 * jnp.bitwise_xor(core, number // 2) + jnp.bitwise_xor(side, number % 2)
            for n in range(2 * WINDOWS):
                half = jnp.bitwise_xor(spot, 1 - n // WINDOWS)
                at = (n % WINDOWS) * window + (2 * place + half) * part
                proj_ref[pl.ds(pl.multiple_of(at, part), part), :] = piece[
                    n * part : (n + 1) * part, :
                ]
        total = None
        for (low, high), act_ref in zip(((0, 1), (0, 2), (1, 3), (2, 3)), refs[4:8]):
            one = lax.dot_general(
                proj_ref[low * window : high * window, :],
                act_ref[...],
                (((0,), (0,)), ((), ())),
                preferred_element_type=F32,
            )
            total = one * one if total is None else total + one * one
        out_ref[...] = total * scale

    return pl.pallas_call(
        kernel,
        grid_spec=pltpu.PrefetchScalarGridSpec(
            num_scalar_prefetch=1,
            grid=(width // size,),
            in_specs=in_specs,
            out_specs=pl.BlockSpec((size, columns), lambda i, w: (start + i, 0)),
            scratch_shapes=[pltpu.VMEM((WINDOWS * window, size), BF16)],
        ),
        out_shape=jax.ShapeDtypeStruct(shape, F32),
        input_output_aliases=alias,
        cost_estimate=cost(
            12 * window * width * columns, 4 * width * columns + 6 * window * width
        ),
    )(*args)


def body(grads, acts, out_basis, in_basis, lengths):
    col = lax.axis_index("col")
    core, side = col % 2, col // 2
    spot = lax.axis_index("seq")
    where = jnp.stack([core, side, spot % 2]).astype(jnp.int32)
    row_size = lax.axis_size("row")
    row = lax.axis_index("row")
    tokens = acts.shape[0] * lax.axis_size("seq") * lax.axis_size("col")
    live = WINDOWS * SEQ_LEN
    part = SEQ_LEN // 4

    def across_core(x):
        return lax.ppermute(x, "col", [(0, 1), (1, 0), (2, 3), (3, 2)])

    def across_side(x):
        return lax.ppermute(x, "col", [(0, 2), (2, 0), (1, 3), (3, 1)])

    def across_pair(x):
        return lax.ppermute(x, "seq", [(0, 1), (1, 0), (2, 3), (3, 2)])

    def across_half(x):
        return lax.ppermute(x, "seq", [(0, 2), (2, 0), (1, 3), (3, 1)])

    ends = jnp.cumsum(lengths)
    order = jnp.arange(live, dtype=jnp.int32)
    past = order[:, None] >= ends[None, :]
    owner = jnp.sum(past.astype(jnp.int32), axis=1)
    token_of = order + jnp.sum(jnp.where(past, SEQ_LEN - lengths[None, :], 0), axis=1)
    split = token_of.reshape(WINDOWS, 4, 2, part // 2).transpose(1, 2, 0, 3)
    split = jnp.where(spot % 2 == 0, split[:, ::-1], split)
    grouped = split.reshape(live)

    def pick(chosen, first, count):
        ids = first + jnp.arange(count, dtype=jnp.int32)
        return (chosen[:, None] == ids[None, :]).astype(BF16)

    share = grads.shape[0]
    if row_size == 2:
        other = lax.ppermute(grads, "row", [(0, 1), (1, 0)])
        packed = dot(pick(grouped, row * share, share), grads) + dot(
            pick(grouped, (1 - row) * share, share), other
        )
    else:
        packed = dot(
            pick(grouped, 0, tokens), lax.all_gather(grads, "row", axis=0, tiled=True)
        )
    packed = packed.astype(BF16)

    def act_sets():
        held_rows = acts.shape[0]
        up, down = [acts], [acts]
        for step in range(3):
            up.append(lax.ppermute(up[-1], "seq", [(i, i + 1) for i in range(step, 3)]))
            down.append(lax.ppermute(down[-1], "seq", [(i + 1, i) for i in range(3 - step)]))
        blocks = [acts]
        for ahead in (1, 2, 3):
            blocks.append(jnp.where(spot + ahead < 4, down[ahead], up[4 - ahead]))
        first = jnp.concatenate([across_side(blocks[0]), across_side(blocks[2])], axis=0)
        second = across_side(jnp.concatenate([blocks[1], blocks[3]], axis=0))
        mine = jnp.concatenate([blocks[0], blocks[2], blocks[1], blocks[3]], axis=0)
        theirs = jnp.concatenate([first, second], axis=0)
        pieces = (mine, theirs, across_core(mine), across_core(theirs))
        place = (spot + jnp.array([0, 2, 1, 3], jnp.int32)) % 4
        ids = jnp.concatenate(
            [
                (
                    (place[:, None] * 4 + 2 * jnp.bitwise_xor(side, n % 2))
                    + jnp.bitwise_xor(core, n // 2)
                )
                * held_rows
                + jnp.arange(held_rows, dtype=jnp.int32)[None, :]
                for n in range(4)
            ]
        ).reshape(tokens)
        act_part = jnp.concatenate([dot(piece, in_basis) for piece in pieces], axis=0)
        if row_size == 2:
            act_sum = act_part + lax.ppermute(act_part, "row", [(0, 1), (1, 0)])
        else:
            act_sum = lax.psum(act_part, "row")
        chosen = (token_of[:, None] == ids[None, :]).astype(BF16)
        act_live = dot(chosen, act_sum.astype(BF16))

        def act_of(seq, low, high):
            span = slice(low * SEQ_LEN, high * SEQ_LEN)
            return jnp.where(owner[span, None] == seq, act_live[span], 0.0).astype(BF16)

        return act_of(0, 0, 1), act_of(1, 0, 2), act_of(2, 1, 3), act_of(3, 2, 3)

    sets = act_sets()
    unit = out_basis.shape[1] // PARTS
    shape = (out_basis.shape[1], in_basis.shape[1])
    rows = live // 4
    half = rows // 2
    held = [{} for _ in PLAN]
    out = None

    def total(*parts):
        value = parts[0].astype(F32)
        for more in parts[1:]:
            value = value + more.astype(F32)
        return value.astype(BF16)

    for chunk, stage in ORDER:
        h = held[chunk]
        width = PLAN[chunk] * unit
        offset = sum(PLAN[:chunk]) * unit
        if stage == 0:
            send, h["away"], h["own"] = project(where, packed, out_basis, offset, width)
        elif stage == 1:
            send = total(h["away"], h["core"][:rows])
        elif stage == 2:
            send = total(h["own"][:half], h["core"][rows : rows + half], h["side"][:half])
        elif stage == 3:
            h["own"] = (h["own"][half:], h["core"][rows + half :], h["side"][half:], h["pair"])
            send = total(*h["own"])
        elif stage == 4:
            send = h["mine"] = total(*h["own"], h["far_pair"])
        elif stage == 5:
            send = h["full"] = jnp.concatenate([h["theirs"], h["mine"]], axis=0)
        elif stage == 7:
            pieces = (h["full"], h["beside"], h["far"], h["last"])
            out = finish(where, pieces, sets, out, shape, offset, width, 1.0 / tokens)
        if stage == 0:
            h["core"] = across_core(send)
        elif stage == 1:
            h["side"] = across_side(send)
        elif stage == 2:
            h["pair"] = across_pair(send)
        elif stage == 3:
            h["far_pair"] = across_half(send)
        elif stage == 4:
            h["theirs"] = across_pair(send)
        elif stage == 5:
            h["beside"] = across_side(send)
            h["far"] = across_core(send)
        elif stage == 6:
            h["last"] = across_core(h["beside"])
    return out


def solution(mesh):
    in_specs = (
        P("row", ("seq", "col")),
        P(("seq", "col"), "row"),
        P(("seq", "col"), "row"),
        P("row", ("seq", "col")),
        P(),
    )
    out_specs = P("row", ("seq", "col"))

    return jax.shard_map(body, mesh=mesh, in_specs=in_specs, out_specs=out_specs, check_vma=False)
```

```python
import jax
import jax.numpy as jnp
from jax import lax
from jax.experimental import pallas as pl
from jax.experimental.pallas import tpu as pltpu
from jax.sharding import PartitionSpec as P


SEQ_LEN = 256
WINDOWS = 3
F32 = jnp.float32
BF16 = jnp.bfloat16
PLAN = (1, 2, 2, 2, 2, 2, 2, 1)
PARTS = 14
ORDER = (
    (0, 0), (1, 0), (0, 1), (2, 0), (1, 1), (0, 2), (3, 0), (0, 3), (2, 1), (3, 1),
    (1, 2), (4, 0), (0, 4), (1, 3), (2, 2), (4, 1), (0, 5), (5, 0), (3, 2), (1, 4),
    (2, 3), (5, 1), (6, 0), (4, 2), (1, 5), (0, 6), (3, 3), (6, 1), (0, 7), (2, 4),
    (4, 3), (7, 0), (3, 4), (7, 1), (5, 2), (2, 5), (1, 6), (1, 7), (4, 4), (3, 5),
    (6, 2), (5, 3), (7, 2), (4, 5), (6, 3), (2, 6), (2, 7), (5, 4), (7, 3), (3, 6),
    (6, 4), (3, 7), (5, 5), (7, 4), (4, 6), (4, 7), (6, 5), (7, 5), (5, 6), (5, 7),
    (6, 6), (6, 7), (7, 6), (7, 7),
)


def block_of(width, offset):
    for size in (512, 256, 128):
        if width % size == 0 and offset % size == 0:
            return size
    return width


def dot(lhs, rhs):
    return jnp.dot(lhs, rhs, preferred_element_type=F32)


def cost(flops, moved):
    return pl.CostEstimate(flops=flops, transcendentals=0, bytes_accessed=moved)


def project(where, lhs, basis, offset, width):
    rows = lhs.shape[0] // 4
    depth = lhs.shape[1]
    size = block_of(width, offset)
    start = offset // size

    def kernel(where_ref, lhs_ref, rhs_ref, send_ref, away_ref, own_ref, acc_ref):
        core, side = where_ref[0], where_ref[1]
        acc_ref[...] = dot(lhs_ref[...], rhs_ref[...])

        def quarter(c, s):
            at = pl.multiple_of((2 * c + s) * rows, rows)
            return acc_ref[pl.ds(at, rows), :]

        send_ref[:rows, :] = quarter(1 - core, 1 - side).astype(BF16)
        send_ref[rows:, :] = quarter(1 - core, side).astype(BF16)
        away_ref[...] = quarter(core, 1 - side).astype(BF16)
        own_ref[...] = quarter(core, side).astype(BF16)

    return pl.pallas_call(
        kernel,
        grid_spec=pltpu.PrefetchScalarGridSpec(
            num_scalar_prefetch=1,
            grid=(width // size,),
            in_specs=[
                pl.BlockSpec((4 * rows, depth), lambda i, w: (0, 0)),
                pl.BlockSpec((depth, size), lambda i, w: (0, start + i)),
            ],
            out_specs=[
                pl.BlockSpec((2 * rows, size), lambda i, w: (0, i)),
                pl.BlockSpec((rows, size), lambda i, w: (0, i)),
                pl.BlockSpec((rows, size), lambda i, w: (0, i)),
            ],
            scratch_shapes=[pltpu.VMEM((4 * rows, size), F32)],
        ),
        out_shape=[
            jax.ShapeDtypeStruct((2 * rows, width), BF16),
            jax.ShapeDtypeStruct((rows, width), BF16),
            jax.ShapeDtypeStruct((rows, width), BF16),
        ],
        compiler_params=pltpu.CompilerParams(vmem_limit_bytes=20 * 2**20),
        cost_estimate=cost(8 * rows * depth * width, 2 * depth * width + 8 * rows * width),
    )(where, lhs, basis)


def finish(where, pieces, acts, out, shape, offset, width, scale):
    size = block_of(width, offset)
    start = offset // size
    window = acts[0].shape[0]
    part = window // 8
    columns = shape[1]
    in_specs = [pl.BlockSpec((p.shape[0], size), lambda i, w: (0, i)) for p in pieces]
    in_specs += [pl.BlockSpec(a.shape, lambda i, w: (0, 0)) for a in acts]
    args = [where, *pieces, *acts]
    alias = {}
    if out is not None:
        in_specs.append(pl.BlockSpec(memory_space=pl.ANY))
        alias = {len(args): 0}
        args.append(out)

    def kernel(where_ref, *refs):
        out_ref, proj_ref = refs[-2:]
        core, side, spot = where_ref[0], where_ref[1], where_ref[2]
        for number, piece in enumerate(refs[:4]):
            place = 2 * jnp.bitwise_xor(core, number // 2) + jnp.bitwise_xor(side, number % 2)
            for n in range(2 * WINDOWS):
                half = jnp.bitwise_xor(spot, 1 - n // WINDOWS)
                at = (n % WINDOWS) * window + (2 * place + half) * part
                proj_ref[pl.ds(pl.multiple_of(at, part), part), :] = piece[
                    n * part : (n + 1) * part, :
                ]
        last = pl.multiple_of(where_ref[3], 16)
        total = None
        for low, act_ref in zip((0, window, 2 * window, last), refs[4:8]):
            one = lax.dot_general(
                proj_ref[pl.ds(low, window), :],
                act_ref[...],
                (((0,), (0,)), ((), ())),
                preferred_element_type=F32,
            )
            total = one * one if total is None else total + one * one
        out_ref[...] = total * scale

    return pl.pallas_call(
        kernel,
        grid_spec=pltpu.PrefetchScalarGridSpec(
            num_scalar_prefetch=1,
            grid=(width // size,),
            in_specs=in_specs,
            out_specs=pl.BlockSpec((size, columns), lambda i, w: (start + i, 0)),
            scratch_shapes=[pltpu.VMEM((WINDOWS * window, size), BF16)],
        ),
        out_shape=jax.ShapeDtypeStruct(shape, F32),
        input_output_aliases=alias,
        compiler_params=pltpu.CompilerParams(vmem_limit_bytes=16 * 2**20),
        cost_estimate=cost(
            8 * window * width * columns, 4 * width * columns + 6 * window * width
        ),
    )(*args)


def body(grads, acts, out_basis, in_basis, lengths):
    col = lax.axis_index("col")
    core, side = col % 2, col // 2
    spot = lax.axis_index("seq")
    row_size = lax.axis_size("row")
    row = lax.axis_index("row")
    tokens = acts.shape[0] * lax.axis_size("seq") * lax.axis_size("col")
    live = WINDOWS * SEQ_LEN
    part = SEQ_LEN // 4

    def across_core(x):
        return lax.ppermute(x, "col", [(0, 1), (1, 0), (2, 3), (3, 2)])

    def across_side(x):
        return lax.ppermute(x, "col", [(0, 2), (2, 0), (1, 3), (3, 1)])

    def across_pair(x):
        return lax.ppermute(x, "seq", [(0, 1), (1, 0), (2, 3), (3, 2)])

    def across_half(x):
        return lax.ppermute(x, "seq", [(0, 2), (2, 0), (1, 3), (3, 1)])

    ids = jnp.arange(lengths.shape[0], dtype=jnp.int32)
    longer = (lengths[None, :] > lengths[:, None]) | (
        (lengths[None, :] == lengths[:, None]) & (ids[None, :] < ids[:, None])
    )
    rank = jnp.sum(longer.astype(jnp.int32), axis=1)
    slot = jnp.where(rank == 2, 3, jnp.where(rank == 3, 2, rank))
    held_by = slot[None, :] == ids[:, None]
    size_of = jnp.sum(jnp.where(held_by, lengths[None, :], 0), axis=1)
    seq_of = jnp.sum(jnp.where(held_by, ids[None, :], 0), axis=1)
    stop = jnp.sum(jnp.where(ids[None, :] <= ids[:, None], size_of[None, :], 0), axis=1)
    order = jnp.arange(live, dtype=jnp.int32)
    past = (order[:, None] >= stop[None, :]).astype(jnp.int32)
    owner = jnp.sum(past, axis=1)
    shift = seq_of * SEQ_LEN - (stop - size_of)
    inside = owner[:, None] == ids[None, :]
    token_of = order + jnp.sum(jnp.where(inside, shift[None, :], 0), axis=1)
    third = stop[1] // 16 * 16
    where = jnp.stack([core, side, spot % 2, third]).astype(jnp.int32)
    split = token_of.reshape(WINDOWS, 4, 2, part // 2).transpose(1, 2, 0, 3)
    split = jnp.where(spot % 2 == 0, split[:, ::-1], split)
    grouped = split.reshape(live)

    def pick(chosen, first, count):
        ids = first + jnp.arange(count, dtype=jnp.int32)
        return (chosen[:, None] == ids[None, :]).astype(BF16)

    share = grads.shape[0]
    if row_size == 2:
        other = lax.ppermute(grads, "row", [(0, 1), (1, 0)])
        packed = dot(pick(grouped, row * share, share), grads) + dot(
            pick(grouped, (1 - row) * share, share), other
        )
    else:
        packed = dot(
            pick(grouped, 0, tokens), lax.all_gather(grads, "row", axis=0, tiled=True)
        )
    packed = packed.astype(BF16)

    def act_sets():
        held_rows = acts.shape[0]
        up, down = [acts], [acts]
        for step in range(3):
            up.append(lax.ppermute(up[-1], "seq", [(i, i + 1) for i in range(step, 3)]))
            down.append(lax.ppermute(down[-1], "seq", [(i + 1, i) for i in range(3 - step)]))
        blocks = [acts]
        for ahead in (1, 2, 3):
            blocks.append(jnp.where(spot + ahead < 4, down[ahead], up[4 - ahead]))
        first = across_side(blocks[0])
        first = jnp.concatenate([first, across_side(blocks[2])], axis=0)
        second = across_side(jnp.concatenate([blocks[1], blocks[3]], axis=0))
        mine = jnp.concatenate([blocks[0], blocks[2], blocks[1], blocks[3]], axis=0)
        theirs = jnp.concatenate([first, second], axis=0)
        pieces = (mine, theirs, across_core(mine), across_core(theirs))
        place = (spot + jnp.array([0, 2, 1, 3], jnp.int32)) % 4
        token_ids = jnp.concatenate(
            [
                (
                    (place[:, None] * 4 + 2 * jnp.bitwise_xor(side, n % 2))
                    + jnp.bitwise_xor(core, n // 2)
                )
                * held_rows
                + jnp.arange(held_rows, dtype=jnp.int32)[None, :]
                for n in range(4)
            ]
        ).reshape(tokens)
        act_part = jnp.concatenate([dot(piece, in_basis) for piece in pieces], axis=0)
        if row_size == 2:
            act_sum = act_part + lax.ppermute(act_part, "row", [(0, 1), (1, 0)])
        else:
            act_sum = lax.psum(act_part, "row")
        chosen = (token_of[:, None] == token_ids[None, :]).astype(BF16)
        act_live = dot(chosen, act_sum.astype(BF16))

        def act_of(slot, low):
            mine = lax.dynamic_slice_in_dim(owner, low, SEQ_LEN)[:, None] == slot
            rows = lax.dynamic_slice_in_dim(act_live, low, SEQ_LEN)
            return jnp.where(mine, rows, 0.0).astype(BF16)

        return act_of(0, 0), act_of(1, SEQ_LEN), act_of(3, 2 * SEQ_LEN), act_of(2, third)

    sets = act_sets()
    unit = out_basis.shape[1] // PARTS
    shape = (out_basis.shape[1], in_basis.shape[1])
    rows = live // 4
    half = rows // 2
    held = [{} for _ in PLAN]
    out = None

    def total(*parts):
        value = parts[0].astype(F32)
        for more in parts[1:]:
            value = value + more.astype(F32)
        return value.astype(BF16)

    for chunk, stage in ORDER:
        h = held[chunk]
        width = PLAN[chunk] * unit
        offset = sum(PLAN[:chunk]) * unit
        if stage == 0:
            send, h["away"], h["own"] = project(where, packed, out_basis, offset, width)
        elif stage == 1:
            send = total(h["away"], h["core"][:rows])
        elif stage == 2:
            send = total(h["own"][:half], h["core"][rows : rows + half], h["side"][:half])
        elif stage == 3:
            h["own"] = (h["own"][half:], h["core"][rows + half :], h["side"][half:], h["pair"])
            send = total(*h["own"])
        elif stage == 4:
            send = h["mine"] = total(*h["own"], h["far_pair"])
        elif stage == 5:
            send = h["full"] = jnp.concatenate([h["theirs"], h["mine"]], axis=0)
        elif stage == 7:
            pieces = (h["full"], h["beside"], h["far"], h["last"])
            out = finish(where, pieces, sets, out, shape, offset, width, 1.0 / tokens)
        if stage == 0:
            h["core"] = across_core(send)
        elif stage == 1:
            h["side"] = across_side(send)
        elif stage == 2:
            h["pair"] = across_pair(send)
        elif stage == 3:
            h["far_pair"] = across_half(send)
        elif stage == 4:
            h["theirs"] = across_pair(send)
        elif stage == 5:
            h["beside"] = across_side(send)
            h["far"] = across_core(send)
        elif stage == 6:
            h["last"] = across_core(h["beside"])
    return out


def solution(mesh):
    in_specs = (
        P("row", ("seq", "col")),
        P(("seq", "col"), "row"),
        P(("seq", "col"), "row"),
        P("row", ("seq", "col")),
        P(),
    )
    out_specs = P("row", ("seq", "col"))

    return jax.shard_map(body, mesh=mesh, in_specs=in_specs, out_specs=out_specs, check_vma=False)
```

```python
import jax
import jax.numpy as jnp
from jax import lax
from jax.experimental import pallas as pl
from jax.experimental.pallas import tpu as pltpu
from jax.sharding import PartitionSpec as P


SEQ_LEN = 256
WINDOWS = 3
F32 = jnp.float32
BF16 = jnp.bfloat16
PLAN = (2, 2, 2, 2, 2, 2, 2)
KINDS = (1, 1, 1, 1, 2, 1, 2)
PARTS = 14
ORDER = (
    (0, 0), (1, 0), (0, 1), (2, 0), (1, 1), (2, 1), (3, 0), (3, 1), (0, 2), (4, 0),
    (0, 3), (1, 2), (5, 0), (2, 2), (4, 1), (5, 1), (1, 3), (0, 4), (6, 0), (3, 2),
    (2, 3), (6, 1), (1, 4), (0, 5), (4, 2), (3, 3), (2, 4), (5, 2), (1, 5), (4, 3),
    (6, 2), (3, 4), (2, 5), (0, 6), (0, 7), (5, 3), (4, 4), (1, 6), (1, 7), (6, 3),
    (3, 5), (2, 6), (2, 7), (5, 4), (4, 5), (6, 4), (5, 5), (3, 6), (3, 7), (6, 5),
    (4, 6), (4, 7), (5, 6), (5, 7), (6, 6), (6, 7),
)


def block_of(width, offset):
    for size in (512, 256, 128):
        if width % size == 0 and offset % size == 0:
            return size
    return width


def dot(lhs, rhs):
    return jnp.dot(lhs, rhs, preferred_element_type=F32)


def cost(flops, moved):
    return pl.CostEstimate(flops=flops, transcendentals=0, bytes_accessed=moved)


def project(where, lhs, basis, offset, width):
    rows = lhs.shape[0] // 4
    depth = lhs.shape[1]
    size = block_of(width, offset)
    start = offset // size

    def kernel(where_ref, lhs_ref, rhs_ref, send_ref, away_ref, own_ref, acc_ref):
        core, side = where_ref[0], where_ref[1]
        acc_ref[...] = dot(lhs_ref[...], rhs_ref[...])

        def quarter(c, s):
            at = pl.multiple_of((2 * c + s) * rows, rows)
            return acc_ref[pl.ds(at, rows), :]

        send_ref[:rows, :] = quarter(1 - core, 1 - side).astype(BF16)
        send_ref[rows:, :] = quarter(1 - core, side).astype(BF16)
        away_ref[...] = quarter(core, 1 - side).astype(BF16)
        own_ref[...] = quarter(core, side).astype(BF16)

    return pl.pallas_call(
        kernel,
        grid_spec=pltpu.PrefetchScalarGridSpec(
            num_scalar_prefetch=1,
            grid=(width // size,),
            in_specs=[
                pl.BlockSpec((4 * rows, depth), lambda i, w: (0, 0)),
                pl.BlockSpec((depth, size), lambda i, w: (0, start + i)),
            ],
            out_specs=[
                pl.BlockSpec((2 * rows, size), lambda i, w: (0, i)),
                pl.BlockSpec((rows, size), lambda i, w: (0, i)),
                pl.BlockSpec((rows, size), lambda i, w: (0, i)),
            ],
            scratch_shapes=[pltpu.VMEM((4 * rows, size), F32)],
        ),
        out_shape=[
            jax.ShapeDtypeStruct((2 * rows, width), BF16),
            jax.ShapeDtypeStruct((rows, width), BF16),
            jax.ShapeDtypeStruct((rows, width), BF16),
        ],
        compiler_params=pltpu.CompilerParams(vmem_limit_bytes=20 * 2**20),
        cost_estimate=cost(8 * rows * depth * width, 2 * depth * width + 8 * rows * width),
    )(where, lhs, basis)


def finish(kind, where, pieces, acts, out, shape, offset, width, scale):
    size = block_of(width, offset)
    start = offset // size
    window = acts[0].shape[0]
    part = window // 8
    columns = shape[1]
    in_specs = [pl.BlockSpec((p.shape[0], size), lambda i, w: (0, i)) for p in pieces]
    in_specs += [pl.BlockSpec(a.shape, lambda i, w: (0, 0)) for a in acts]
    args = [where, *pieces, *acts]
    alias = {}
    if out is not None:
        in_specs.append(pl.BlockSpec(memory_space=pl.ANY))
        alias = {len(args): 0}
        args.append(out)

    def kernel(where_ref, *refs):
        out_ref, proj_ref = refs[-2:]
        core, side, spot = where_ref[0], where_ref[1], where_ref[2]
        for number, piece in enumerate(refs[:4]):
            its_core = jnp.bitwise_xor(core, number // 2)
            for n in range(2 * WINDOWS):
                group = n // WINDOWS
                if kind == 1:
                    its_side, half = side ^ (number % 2), spot ^ (1 - group)
                else:
                    its_side, half = side ^ group, spot ^ (number % 2)
                at = (n % WINDOWS) * window + (4 * its_core + 2 * its_side + half) * part
                proj_ref[pl.ds(pl.multiple_of(at, part), part), :] = piece[
                    n * part : (n + 1) * part, :
                ]
        last = pl.multiple_of(where_ref[3], 16)
        total = None
        for low, act_ref in zip((0, window, 2 * window, last), refs[4:8]):
            one = lax.dot_general(
                proj_ref[pl.ds(low, window), :],
                act_ref[...],
                (((0,), (0,)), ((), ())),
                preferred_element_type=F32,
            )
            total = one * one if total is None else total + one * one
        out_ref[...] = total * scale

    return pl.pallas_call(
        kernel,
        grid_spec=pltpu.PrefetchScalarGridSpec(
            num_scalar_prefetch=1,
            grid=(width // size,),
            in_specs=in_specs,
            out_specs=pl.BlockSpec((size, columns), lambda i, w: (start + i, 0)),
            scratch_shapes=[pltpu.VMEM((WINDOWS * window, size), BF16)],
        ),
        out_shape=jax.ShapeDtypeStruct(shape, F32),
        input_output_aliases=alias,
        compiler_params=pltpu.CompilerParams(vmem_limit_bytes=16 * 2**20),
        cost_estimate=cost(
            8 * window * width * columns, 4 * width * columns + 6 * window * width
        ),
    )(*args)


def body(grads, acts, out_basis, in_basis, lengths):
    col = lax.axis_index("col")
    core, side = col % 2, col // 2
    spot = lax.axis_index("seq")
    row_size = lax.axis_size("row")
    row = lax.axis_index("row")
    tokens = acts.shape[0] * lax.axis_size("seq") * lax.axis_size("col")
    live = WINDOWS * SEQ_LEN
    part = SEQ_LEN // 4

    def across_core(x):
        return lax.ppermute(x, "col", [(0, 1), (1, 0), (2, 3), (3, 2)])

    def across_side(x):
        return lax.ppermute(x, "col", [(0, 2), (2, 0), (1, 3), (3, 1)])

    def across_pair(x):
        return lax.ppermute(x, "seq", [(0, 1), (1, 0), (2, 3), (3, 2)])

    def across_half(x):
        return lax.ppermute(x, "seq", [(0, 2), (2, 0), (1, 3), (3, 1)])

    ids = jnp.arange(lengths.shape[0], dtype=jnp.int32)
    longer = (lengths[None, :] > lengths[:, None]) | (
        (lengths[None, :] == lengths[:, None]) & (ids[None, :] < ids[:, None])
    )
    rank = jnp.sum(longer.astype(jnp.int32), axis=1)
    slot = jnp.where(rank == 2, 3, jnp.where(rank == 3, 2, rank))
    held_by = slot[None, :] == ids[:, None]
    size_of = jnp.sum(jnp.where(held_by, lengths[None, :], 0), axis=1)
    seq_of = jnp.sum(jnp.where(held_by, ids[None, :], 0), axis=1)
    stop = jnp.sum(jnp.where(ids[None, :] <= ids[:, None], size_of[None, :], 0), axis=1)
    order = jnp.arange(live, dtype=jnp.int32)
    past = (order[:, None] >= stop[None, :]).astype(jnp.int32)
    owner = jnp.sum(past, axis=1)
    shift = seq_of * SEQ_LEN - (stop - size_of)
    inside = owner[:, None] == ids[None, :]
    token_of = order + jnp.sum(jnp.where(inside, shift[None, :], 0), axis=1)
    third = stop[1] // 16 * 16
    where = jnp.stack([core, side, spot % 2, third]).astype(jnp.int32)
    split = token_of.reshape(WINDOWS, 4, 2, part // 2).transpose(1, 2, 0, 3)
    split = jnp.where(spot % 2 == 0, split[:, ::-1], split)
    grouped = split.reshape(live)

    def pick(chosen, first, count):
        ids = first + jnp.arange(count, dtype=jnp.int32)
        return (chosen[:, None] == ids[None, :]).astype(BF16)

    share = grads.shape[0]
    if row_size == 2:
        other = lax.ppermute(grads, "row", [(0, 1), (1, 0)])
        packed = dot(pick(grouped, row * share, share), grads) + dot(
            pick(grouped, (1 - row) * share, share), other
        )
    else:
        packed = dot(
            pick(grouped, 0, tokens), lax.all_gather(grads, "row", axis=0, tiled=True)
        )
    packed = packed.astype(BF16)

    def act_sets():
        held_rows = acts.shape[0]
        up, down = [acts], [acts]
        for step in range(3):
            up.append(lax.ppermute(up[-1], "seq", [(i, i + 1) for i in range(step, 3)]))
            down.append(lax.ppermute(down[-1], "seq", [(i + 1, i) for i in range(3 - step)]))
        blocks = [acts]
        for ahead in (1, 2, 3):
            blocks.append(jnp.where(spot + ahead < 4, down[ahead], up[4 - ahead]))
        first = across_side(blocks[0])
        second = across_side(blocks[2])
        third_part = across_side(jnp.concatenate([blocks[1], blocks[3]], axis=0))
        mine = jnp.concatenate([blocks[0], blocks[2], blocks[1], blocks[3]], axis=0)
        theirs = jnp.concatenate([first, second, third_part], axis=0)
        mine_far = across_core(mine)
        theirs_far = across_core(theirs)
        pieces = (mine, theirs, mine_far, theirs_far)
        seats = []
        for n in range(4):
            for ahead in (0, 2, 1, 3):
                seats.append((spot + ahead) % 4 * 4 + 2 * (side ^ (n % 2)) + (core ^ (n // 2)))
        token_ids = (
            jnp.stack(seats)[:, None] * held_rows
            + jnp.arange(held_rows, dtype=jnp.int32)[None, :]
        ).reshape(tokens)
        act_part = jnp.concatenate([dot(piece, in_basis) for piece in pieces], axis=0)
        if row_size == 2:
            other = lax.ppermute(act_part, "row", [(0, 1), (1, 0)])
            act_sum = act_part + other
        else:
            act_sum = lax.psum(act_part, "row")
        chosen = (token_of[:, None] == token_ids[None, :]).astype(BF16)
        act_live = dot(chosen, act_sum.astype(BF16))

        def act_of(slot, low):
            mine = lax.dynamic_slice_in_dim(owner, low, SEQ_LEN)[:, None] == slot
            rows = lax.dynamic_slice_in_dim(act_live, low, SEQ_LEN)
            return jnp.where(mine, rows, 0.0).astype(BF16)

        return act_of(0, 0), act_of(1, SEQ_LEN), act_of(3, 2 * SEQ_LEN), act_of(2, third)

    sets = act_sets()
    unit = out_basis.shape[1] // PARTS
    shape = (out_basis.shape[1], in_basis.shape[1])
    rows = live // 4
    half = rows // 2
    held = [{} for _ in PLAN]
    out = None

    def total(*parts):
        value = parts[0].astype(F32)
        for more in parts[1:]:
            value = value + more.astype(F32)
        return value.astype(BF16)

    for chunk, stage in ORDER:
        h = held[chunk]
        kind = KINDS[chunk]
        width = PLAN[chunk] * unit
        offset = sum(PLAN[:chunk]) * unit
        if stage == 0:
            send, h["away"], h["own"] = project(where, packed, out_basis, offset, width)
        elif stage == 1:
            send = total(h["away"], h["core"][:rows])
        elif stage == 2:
            send = total(h["own"][:half], h["core"][rows : rows + half], h["side"][:half])
        elif stage == 3:
            h["own"] = (h["own"][half:], h["core"][rows + half :], h["side"][half:], h["pair"])
            send = total(*h["own"])
        elif stage == 4:
            send = h["mine"] = total(*h["own"], h["far_pair"])
        elif stage == 5 and kind == 1:
            send = h["full"] = jnp.concatenate([h["theirs"], h["mine"]], axis=0)
        elif stage == 5:
            send = h["full"] = jnp.concatenate([h["mine"], h["theirs"]], axis=0)
        elif stage == 7:
            pieces = (h["full"], h["beside"], h["far"], h["last"])
            out = finish(
                kind, where, pieces, sets, out, shape, offset, width, 1.0 / tokens
            )
        if stage == 0:
            h["core"] = across_core(send)
        elif stage == 1:
            h["side"] = across_side(send)
        elif stage == 2:
            h["pair"] = across_pair(send)
        elif stage == 3:
            h["far_pair"] = across_half(send)
        elif stage == 4:
            move = across_pair if kind == 1 else across_side
            h["theirs"] = move(send)
        elif stage == 5:
            move = across_side if kind == 1 else across_pair
            h["beside"] = move(send)
            h["far"] = across_core(send)
        elif stage == 6:
            h["last"] = across_core(h["beside"])
    return out


def solution(mesh):
    in_specs = (
        P("row", ("seq", "col")),
        P(("seq", "col"), "row"),
        P(("seq", "col"), "row"),
        P("row", ("seq", "col")),
        P(),
    )
    out_specs = P("row", ("seq", "col"))

    return jax.shard_map(body, mesh=mesh, in_specs=in_specs, out_specs=out_specs, check_vma=False)
```

```python
import jax
import jax.numpy as jnp
from jax import lax
from jax.experimental import pallas as pl
from jax.experimental.pallas import tpu as pltpu
from jax.sharding import PartitionSpec as P


SEQ_LEN = 256
WINDOWS = 3
F32 = jnp.float32
BF16 = jnp.bfloat16
PLAN = (2, 2, 2, 2, 2, 2, 2)
KINDS = (1, 1, 1, 1, 2, 1, 2)
PARTS = 14
ORDER = (
    (0, 0), (1, 0), (0, 1), (2, 0), (1, 1), (2, 1), (3, 0), (0, 2), (3, 1), (4, 0),
    (0, 3), (1, 2), (4, 1), (5, 0), (2, 2), (6, 0), (1, 3), (0, 4), (3, 2), (2, 3),
    (5, 1), (6, 1), (0, 5), (1, 4), (4, 2), (3, 3), (2, 4), (5, 2), (1, 5), (4, 3),
    (6, 2), (3, 4), (2, 5), (0, 6), (0, 7), (5, 3), (4, 4), (1, 6), (1, 7), (6, 3),
    (3, 5), (2, 6), (2, 7), (5, 4), (4, 5), (6, 4), (5, 5), (3, 6), (3, 7), (6, 5),
    (4, 6), (4, 7), (5, 6), (5, 7), (6, 6), (6, 7),
)


def block_of(width, offset):
    for size in (512, 256, 128):
        if width % size == 0 and offset % size == 0:
            return size
    return width


def dot(lhs, rhs):
    return jnp.dot(lhs, rhs, preferred_element_type=F32)


def cost(flops, moved):
    return pl.CostEstimate(flops=flops, transcendentals=0, bytes_accessed=moved)


def project(where, lhs, basis, offset, width):
    rows = lhs.shape[0] // 4
    depth = lhs.shape[1]
    size = block_of(width, offset)
    start = offset // size

    def kernel(where_ref, lhs_ref, rhs_ref, send_ref, away_ref, own_ref, acc_ref):
        core, side = where_ref[0], where_ref[1]
        acc_ref[...] = dot(lhs_ref[...], rhs_ref[...])

        def quarter(c, s):
            at = pl.multiple_of((2 * c + s) * rows, rows)
            return acc_ref[pl.ds(at, rows), :]

        send_ref[:rows, :] = quarter(1 - core, 1 - side).astype(BF16)
        send_ref[rows:, :] = quarter(1 - core, side).astype(BF16)
        away_ref[...] = quarter(core, 1 - side).astype(BF16)
        own_ref[...] = quarter(core, side).astype(BF16)

    return pl.pallas_call(
        kernel,
        grid_spec=pltpu.PrefetchScalarGridSpec(
            num_scalar_prefetch=1,
            grid=(width // size,),
            in_specs=[
                pl.BlockSpec((4 * rows, depth), lambda i, w: (0, 0)),
                pl.BlockSpec((depth, size), lambda i, w: (0, start + i)),
            ],
            out_specs=[
                pl.BlockSpec((2 * rows, size), lambda i, w: (0, i)),
                pl.BlockSpec((rows, size), lambda i, w: (0, i)),
                pl.BlockSpec((rows, size), lambda i, w: (0, i)),
            ],
            scratch_shapes=[pltpu.VMEM((4 * rows, size), F32)],
        ),
        out_shape=[
            jax.ShapeDtypeStruct((2 * rows, width), BF16),
            jax.ShapeDtypeStruct((rows, width), BF16),
            jax.ShapeDtypeStruct((rows, width), BF16),
        ],
        compiler_params=pltpu.CompilerParams(vmem_limit_bytes=20 * 2**20),
        cost_estimate=cost(8 * rows * depth * width, 2 * depth * width + 8 * rows * width),
    )(where, lhs, basis)


def finish(kind, where, pieces, acts, out, shape, offset, width, scale):
    size = block_of(width, offset)
    start = offset // size
    window = acts[0].shape[0]
    part = window // 8
    columns = shape[1]
    in_specs = [pl.BlockSpec((p.shape[0], size), lambda i, w: (0, i)) for p in pieces]
    in_specs += [pl.BlockSpec(a.shape, lambda i, w: (0, 0)) for a in acts]
    args = [where, *pieces, *acts]
    alias = {}
    if out is not None:
        in_specs.append(pl.BlockSpec(memory_space=pl.ANY))
        alias = {len(args): 0}
        args.append(out)

    def kernel(where_ref, *refs):
        out_ref, proj_ref = refs[-2:]
        core, side, spot = where_ref[0], where_ref[1], where_ref[2]
        for number, piece in enumerate(refs[:4]):
            its_core = jnp.bitwise_xor(core, number // 2)
            for n in range(2 * WINDOWS):
                group = n // WINDOWS
                if kind == 1:
                    its_side, half = side ^ (number % 2), spot ^ (1 - group)
                else:
                    its_side, half = side ^ group, spot ^ (number % 2)
                at = (n % WINDOWS) * window + (4 * its_core + 2 * its_side + half) * part
                proj_ref[pl.ds(pl.multiple_of(at, part), part), :] = piece[
                    n * part : (n + 1) * part, :
                ]
        last = pl.multiple_of(where_ref[3], 16)
        total = None
        for low, act_ref in zip((0, window, 2 * window, last), refs[4:8]):
            one = lax.dot_general(
                proj_ref[pl.ds(low, window), :],
                act_ref[...],
                (((0,), (0,)), ((), ())),
                preferred_element_type=F32,
            )
            total = one * one if total is None else total + one * one
        out_ref[...] = total * scale

    return pl.pallas_call(
        kernel,
        grid_spec=pltpu.PrefetchScalarGridSpec(
            num_scalar_prefetch=1,
            grid=(width // size,),
            in_specs=in_specs,
            out_specs=pl.BlockSpec((size, columns), lambda i, w: (start + i, 0)),
            scratch_shapes=[pltpu.VMEM((WINDOWS * window, size), BF16)],
        ),
        out_shape=jax.ShapeDtypeStruct(shape, F32),
        input_output_aliases=alias,
        compiler_params=pltpu.CompilerParams(vmem_limit_bytes=16 * 2**20),
        cost_estimate=cost(
            8 * window * width * columns, 4 * width * columns + 6 * window * width
        ),
    )(*args)


def body(grads, acts, out_basis, in_basis, lengths):
    col = lax.axis_index("col")
    core, side = col % 2, col // 2
    spot = lax.axis_index("seq")
    row_size = lax.axis_size("row")
    row = lax.axis_index("row")
    tokens = acts.shape[0] * lax.axis_size("seq") * lax.axis_size("col")
    live = WINDOWS * SEQ_LEN
    part = SEQ_LEN // 4

    def across_core(x):
        return lax.ppermute(x, "col", [(0, 1), (1, 0), (2, 3), (3, 2)])

    def across_side(x):
        return lax.ppermute(x, "col", [(0, 2), (2, 0), (1, 3), (3, 1)])

    def across_pair(x):
        return lax.ppermute(x, "seq", [(0, 1), (1, 0), (2, 3), (3, 2)])

    def across_half(x):
        return lax.ppermute(x, "seq", [(0, 2), (2, 0), (1, 3), (3, 1)])

    ids = jnp.arange(lengths.shape[0], dtype=jnp.int32)
    longer = (lengths[None, :] > lengths[:, None]) | (
        (lengths[None, :] == lengths[:, None]) & (ids[None, :] < ids[:, None])
    )
    rank = jnp.sum(longer.astype(jnp.int32), axis=1)
    slot = jnp.where(rank == 2, 3, jnp.where(rank == 3, 2, rank))
    held_by = slot[None, :] == ids[:, None]
    size_of = jnp.sum(jnp.where(held_by, lengths[None, :], 0), axis=1)
    seq_of = jnp.sum(jnp.where(held_by, ids[None, :], 0), axis=1)
    stop = jnp.sum(jnp.where(ids[None, :] <= ids[:, None], size_of[None, :], 0), axis=1)
    order = jnp.arange(live, dtype=jnp.int32)
    past = (order[:, None] >= stop[None, :]).astype(jnp.int32)
    owner = jnp.sum(past, axis=1)
    shift = seq_of * SEQ_LEN - (stop - size_of)
    inside = owner[:, None] == ids[None, :]
    token_of = order + jnp.sum(jnp.where(inside, shift[None, :], 0), axis=1)
    third = stop[1] // 16 * 16
    where = jnp.stack([core, side, spot % 2, third]).astype(jnp.int32)
    split = token_of.reshape(WINDOWS, 4, 2, part // 2).transpose(1, 2, 0, 3)
    split = jnp.where(spot % 2 == 0, split[:, ::-1], split)
    grouped = split.reshape(live)

    def pick(chosen, first, count):
        ids = first + jnp.arange(count, dtype=jnp.int32)
        return (chosen[:, None] == ids[None, :]).astype(BF16)

    share = grads.shape[0]
    if row_size == 2:
        other = lax.ppermute(grads, "row", [(0, 1), (1, 0)])
        packed = dot(pick(grouped, row * share, share), grads) + dot(
            pick(grouped, (1 - row) * share, share), other
        )
    else:
        packed = dot(
            pick(grouped, 0, tokens), lax.all_gather(grads, "row", axis=0, tiled=True)
        )
    packed = packed.astype(BF16)

    def act_sets():
        held_rows = acts.shape[0]
        up, down = [acts], [acts]
        for step in range(3):
            up.append(lax.ppermute(up[-1], "seq", [(i, i + 1) for i in range(step, 3)]))
            down.append(lax.ppermute(down[-1], "seq", [(i + 1, i) for i in range(3 - step)]))
        blocks = [acts]
        for ahead in (1, 2, 3):
            blocks.append(jnp.where(spot + ahead < 4, down[ahead], up[4 - ahead]))
        first = across_side(blocks[0])
        second = across_side(blocks[2])
        third_part = across_side(jnp.concatenate([blocks[1], blocks[3]], axis=0))
        mine = jnp.concatenate([blocks[0], blocks[2], blocks[1], blocks[3]], axis=0)
        theirs = jnp.concatenate([first, second, third_part], axis=0)
        mine_far = across_core(mine)
        theirs_far = across_core(theirs)
        pieces = (mine, theirs, mine_far, theirs_far)
        seats = []
        for n in range(4):
            for ahead in (0, 2, 1, 3):
                seats.append((spot + ahead) % 4 * 4 + 2 * (side ^ (n % 2)) + (core ^ (n // 2)))
        token_ids = (
            jnp.stack(seats)[:, None] * held_rows
            + jnp.arange(held_rows, dtype=jnp.int32)[None, :]
        ).reshape(tokens)
        act_part = jnp.concatenate([dot(piece, in_basis) for piece in pieces], axis=0)
        if row_size == 2:
            other = lax.ppermute(act_part, "row", [(0, 1), (1, 0)])
            act_sum = act_part + other
        else:
            act_sum = lax.psum(act_part, "row")
        chosen = (token_of[:, None] == token_ids[None, :]).astype(BF16)
        act_live = dot(chosen, act_sum.astype(BF16))

        def act_of(slot, low):
            mine = lax.dynamic_slice_in_dim(owner, low, SEQ_LEN)[:, None] == slot
            rows = lax.dynamic_slice_in_dim(act_live, low, SEQ_LEN)
            return jnp.where(mine, rows, 0.0).astype(BF16)

        return act_of(0, 0), act_of(1, SEQ_LEN), act_of(3, 2 * SEQ_LEN), act_of(2, third)

    sets = act_sets()
    unit = out_basis.shape[1] // PARTS
    shape = (out_basis.shape[1], in_basis.shape[1])
    rows = live // 4
    half = rows // 2
    held = [{} for _ in PLAN]
    out = None

    def total(*parts):
        value = parts[0].astype(F32)
        for more in parts[1:]:
            value = value + more.astype(F32)
        return value.astype(BF16)

    for chunk, stage in ORDER:
        h = held[chunk]
        kind = KINDS[chunk]
        width = PLAN[chunk] * unit
        offset = sum(PLAN[:chunk]) * unit
        if stage == 0:
            send, h["away"], h["own"] = project(where, packed, out_basis, offset, width)
        elif stage == 1:
            send = total(h["away"], h["core"][:rows])
        elif stage == 2:
            send = total(h["own"][:half], h["core"][rows : rows + half], h["side"][:half])
        elif stage == 3:
            h["own"] = (h["own"][half:], h["core"][rows + half :], h["side"][half:], h["pair"])
            send = total(*h["own"])
        elif stage == 4:
            send = h["mine"] = total(*h["own"], h["far_pair"])
        elif stage == 5 and kind == 1:
            send = h["full"] = jnp.concatenate([h["theirs"], h["mine"]], axis=0)
        elif stage == 5:
            send = h["full"] = jnp.concatenate([h["mine"], h["theirs"]], axis=0)
        elif stage == 7:
            pieces = (h["full"], h["beside"], h["far"], h["last"])
            out = finish(
                kind, where, pieces, sets, out, shape, offset, width, 1.0 / tokens
            )
        if stage == 0:
            h["core"] = across_core(send)
        elif stage == 1:
            h["side"] = across_side(send)
        elif stage == 2:
            h["pair"] = across_pair(send)
        elif stage == 3:
            h["far_pair"] = across_half(send)
        elif stage == 4:
            move = across_pair if kind == 1 else across_side
            h["theirs"] = move(send)
        elif stage == 5:
            move = across_side if kind == 1 else across_pair
            h["beside"] = move(send)
            h["far"] = across_core(send)
        elif stage == 6:
            h["last"] = across_core(h["beside"])
    return out


def solution(mesh):
    in_specs = (
        P("row", ("seq", "col")),
        P(("seq", "col"), "row"),
        P(("seq", "col"), "row"),
        P("row", ("seq", "col")),
        P(),
    )
    out_specs = P("row", ("seq", "col"))

    return jax.shard_map(body, mesh=mesh, in_specs=in_specs, out_specs=out_specs, check_vma=False)
```
